512 devices in a mesh: mem: 64 (over y_hi, x, z), lat: 8 (over y_lo, core).
Axes of the slice: x: 4, y: 8 (y_hi: 2, y_lo: 4; y = y_hi * 4 + y_lo), z: 8, core: 2. Of those that a mesh axis runs over, the one named last changes fastest.
Arguments:
- ensemble: bfloat16 [64, 512, 3072], P('mem', 'lat'), may hold values from -0.75 to 0.75
- alpha: float32 [64, 512, 3072], P('mem', 'lat'), may hold values from -6 to 6
- background: float32 [512, 3072], P('lat'), may hold values from -4 to 4
- east_coef: float32 [512, 3072], P('lat'), may hold values from 0.03 to 0.24
- north_coef: float32 [512, 3072], P('lat'), may hold values from 0.03 to 0.24
- obs_cell: int32 [32768], P('lat'), may hold values from 0 to 1572863, as said below
- obs_type: int32 [32768], P('lat'), may hold values from 0 to 2
- obs_value: float32 [32768], P('lat'), may hold values from -5 to 5
- obs_weight: float32 [32768], P('lat'), may hold values from 1 to 8
Outputs:
- gradient: float32 [64, 512, 3072], P('mem', 'lat')
The draws below stay inside these ranges and needn't reach their ends.
Inputs may be any that keep to these rules, and one draw needn't show every extreme that they name: `obs_cell`: observation i lies in latitude row (i // 4096) * 64 + (i % 4096) // 64; its column is arbitrary, and a cell may hold several observations.
All inputs are finite; a program needn't handle non-finite values.
Results may differ from the reference program's by a relative error of at most 0.0003.
Values sent between devices are 32-bit elements; how exact they have to be, the bound alone decides.
A program may use at most 64 MiB of HBM per device.

```python
import math
import jax
import jax.numpy as jnp
from jax import lax

NLON = 3072
LAT_DEV = 64
OBS_DEV = 4096
PASSES = 4
MEMBERS = 64
NLAT = 512
NOBS = 32768


def draw_obs_cell(key, part):
    index = jnp.arange(NOBS, dtype=jnp.int32)
    slab_of = index // OBS_DEV
    row_in = index % OBS_DEV // (OBS_DEV // LAT_DEV)
    column = jax.random.randint(key, (NOBS,), 0, NLON, dtype=jnp.int32)
    return (slab_of * LAT_DEV + row_in) * NLON + column


def touch_ends(array, rng, least, high):
    longest = array.shape.index(max(array.shape))
    spots = []
    for shift in (0, 1):
        where = [jax.random.randint(jax.random.fold_in(rng, axis), (), 0, length) for axis, length in enumerate(array.shape)]
        where[longest] = (where[longest] + shift) % array.shape[longest]
        spots.append(tuple(where))
    return array.at[spots[0]].set(least).at[spots[1]].set(high)


def block_scale(rng, shape, cuts, least, largest):
    factor_of = 1.0
    for axis_at, blocks in cuts:
        draws = jax.random.uniform(jax.random.fold_in(jax.random.fold_in(rng, 6), axis_at), (blocks,), jnp.float32, least / len(cuts), largest / len(cuts))
        factor_of = factor_of * jnp.repeat(jnp.exp(draws), shape[axis_at] // blocks).reshape((-1,) + (1,) * (len(shape) - 1 - axis_at))
    return factor_of


def scatter_about(stream_key, extent, width, limit, shards=(), held_as=jnp.bfloat16):
    loudness = block_scale(stream_key, extent, shards, -0.22, 0.18) if shards else 1.0
    values = jax.random.normal(stream_key, extent, jnp.float32) * width * loudness
    return jnp.minimum(jnp.maximum(values, -limit), limit).astype(held_as)


def setup_inputs(seed: int = 0) -> dict:
    seeds = jax.random.split(jax.random.key(seed), 10)
    ensemble = scatter_about(seeds[0], (MEMBERS, NLAT, NLON), MEMBERS ** -0.5, 0.75, ((0, 64), (1, 8)))
    alpha = scatter_about(seeds[1], (MEMBERS, NLAT, NLON), 1.0, 6.0, ((0, 64), (1, 8)), jnp.float32)
    background = scatter_about(seeds[2], (NLAT, NLON), 1.0, 4.0, ((0, 8),), jnp.float32)
    east_coef = jnp.clip(0.03 + 0.21 * jax.random.uniform(seeds[3], (NLAT, NLON), jnp.float32) ** block_scale(seeds[3], (NLAT, NLON), ((0, 8),), -0.2, 0.2), 0.03, 0.24)
    north_coef = jnp.clip(0.03 + 0.21 * jax.random.uniform(seeds[4], (NLAT, NLON), jnp.float32) ** block_scale(seeds[4], (NLAT, NLON), ((0, 8),), -0.2, 0.2), 0.03, 0.24)
    obs_cell = draw_obs_cell(jax.random.fold_in(seeds[9], 71), 0)
    obs_type = touch_ends(jax.random.randint(seeds[6], (NOBS,), 0, 3), jax.random.fold_in(seeds[6], 1), 0, 2).astype(jnp.int32)
    obs_value = scatter_about(seeds[7], (NOBS,), 1.0, 5.0, ((0, 8),), jnp.float32)
    obs_weight = jnp.clip(jnp.exp(math.log(8.0) - 2.0794415 * jax.random.uniform(seeds[8], (NOBS,), jnp.float32) ** block_scale(seeds[8], (NOBS,), ((0, 8),), -0.2, 0.2)), 1.0, 8.0)
    return {"ensemble": ensemble, "alpha": alpha, "background": background, "east_coef": east_coef, "north_coef": north_coef, "obs_cell": obs_cell, "obs_type": obs_type, "obs_value": obs_value, "obs_weight": obs_weight}


def diffuse(field, east_coef, north_coef, south_coef, above, below):
    to_east = jnp.roll(field, -1, axis=1)
    to_west = jnp.roll(field, 1, axis=1)
    west_coef = jnp.roll(east_coef, 1, axis=1)
    return (field + east_coef * (to_east - field) + west_coef * (to_west - field)
            + north_coef * (above - field) + south_coef * (below - field))


def smooth(field, east_coef, north_coef):
    zero_row = jnp.zeros_like(field[:1])
    south_coef = jnp.concatenate([zero_row, north_coef[:-1]], 0)
    for repeat in range(PASSES):
        above = jnp.concatenate([field[1:], zero_row], 0)
        below = jnp.concatenate([zero_row, field[:-1]], 0)
        field = diffuse(field, east_coef, north_coef, south_coef, above, below)
    return field


def observe(at_obs, obs_type, obs_value, obs_weight):
    mapped = jnp.where(obs_type == 0, at_obs,
                       jnp.where(obs_type == 1, 0.5 * at_obs * jnp.abs(at_obs), 0.5 * jax.nn.softplus(2.0 * at_obs)))
    slope = jnp.where(obs_type == 0, jnp.ones_like(at_obs),
                      jnp.where(obs_type == 1, jnp.abs(at_obs), jax.nn.sigmoid(2.0 * at_obs)))
    return obs_weight * (mapped - obs_value) * slope


def reference(ensemble, alpha, background, east_coef, north_coef, obs_cell, obs_type, obs_value, obs_weight):
    def accumulate(total, pair):
        member, control = pair
        return total + member.astype(jnp.float32) * smooth(control, east_coef, north_coef), None

    increment, _ = lax.scan(accumulate, jnp.zeros_like(background), (ensemble, alpha))
    state = (background + increment).reshape(-1)
    at_obs = state[obs_cell]
    misfit = observe(at_obs, obs_type, obs_value, obs_weight)
    forcing = jnp.zeros_like(state).at[obs_cell].add(misfit).reshape(background.shape)

    def adjoint(pair):
        member, control = pair
        return smooth(member.astype(jnp.float32) * forcing, east_coef, north_coef) + control

    return lax.map(adjoint, (ensemble, alpha))
```

```python
import functools

import jax
import jax.numpy as jnp
from jax import lax
from jax.experimental import pallas as pl
from jax.experimental.pallas import tpu as pltpu
from jax.sharding import PartitionSpec as P

PASSES = 4
AXES = (("y", 2), ("x", 4), ("z", 8))
ORDERS = ("zxy", "xyz", "yzx", "zyx")
LANES = 128
MESH = pl.DeviceIdType.MESH


def iota(shape, dim):
    return lax.broadcasted_iota(jnp.int32, shape, dim)


def lane_gather(values, lanes):
    return jnp.take_along_axis(values, lanes, axis=1, mode="promise_in_bounds")


def kernel(
    axes, alpha_hbm, member_hbm, back_hbm, east_hbm, north_hbm, cell_hbm, kind_hbm, value_hbm, weight_hbm,
    out_ref,
    field, east, north, ping, pong, member, back,
    cell_raw, kind_raw, value_raw, weight_raw, rows_int, rows_float,
    col_tile, key_tile, wgt_tile, wv_tile, sums, member_at, back_at, rep_tile, inverse,
    col_up, col_down, use_tile, use_up, use_down, part, inbox,
    load_sem, halo_send, halo_recv, stage_send, stage_recv,
):
    rows = alpha_hbm.shape[1]
    columns = alpha_hbm.shape[2]
    blocks = columns // LANES
    own = rows // 8
    half = own // 2
    per_row = LANES // 2
    lat = lax.axis_index("lat")
    lats = lax.axis_size("lat")
    mem = lax.axis_index("mem")
    has_up = lat < lats - 1
    has_down = lat > 0

    place = {}
    stride = {}
    rest = mem
    step = 1
    for name, size in reversed(axes):
        place[name] = lax.rem(rest, size)
        stride[name] = step
        rest = rest // size
        step = step * size
    sizes = dict(axes)

    def peer(name, ahead):
        there = lax.rem(place[name] + ahead, sizes[name])
        return {"mem": mem + (there - place[name]) * stride[name], "lat": lat}

    up = {"mem": mem, "lat": lat + 1}
    down = {"mem": mem, "lat": lat - 1}

    barrier = pltpu.get_barrier_semaphore()
    met = 0
    for name, size in axes:
        for ahead in range(1, size):
            pl.semaphore_signal(barrier, inc=1, device_id=peer(name, ahead), device_id_type=MESH)
            met += 1

    @pl.when(has_up)
    def _():
        pl.semaphore_signal(barrier, inc=1, device_id=up, device_id_type=MESH)

    @pl.when(has_down)
    def _():
        pl.semaphore_signal(barrier, inc=1, device_id=down, device_id_type=MESH)

    loads = [
        pltpu.make_async_copy(source, target, load_sem.at[index])
        for index, (source, target) in enumerate((
            (cell_hbm, cell_raw), (kind_hbm, kind_raw), (value_hbm, value_raw), (weight_hbm, weight_raw),
            (member_hbm.at[0], member), (alpha_hbm.at[0], field.at[pl.ds(0, rows)]),
            (east_hbm, east.at[pl.ds(0, rows)]), (north_hbm, north.at[pl.ds(0, rows)]), (back_hbm, back),
        ))
    ]
    for load in loads:
        load.start()

    tile = (8, LANES)
    lane = iota(tile, 1)
    sub = iota(tile, 0)
    low = lane < per_row

    zeros4 = jnp.zeros((4, columns), jnp.float32)

    @pl.when(jnp.logical_not(has_up))
    def _():
        for ref in (field, east, north):
            ref[rows : rows + 4, :] = zeros4
        col_up[...] = jnp.zeros(tile, jnp.int32)
        use_up[...] = jnp.zeros(tile, jnp.float32)

    @pl.when(jnp.logical_not(has_down))
    def _():
        for ref in (field, east, north):
            ref[rows + 4 : rows + 8, :] = zeros4
        col_down[...] = jnp.zeros(tile, jnp.int32)
        use_down[...] = jnp.zeros(tile, jnp.float32)

    def to_tiles(raw):
        rows_of = rows_int if raw.dtype == jnp.int32 else rows_float
        rows_of[pl.ds(0, rows // 2, stride=2), :] = raw
        rows_of[pl.ds(1, rows // 2, stride=2), :] = pltpu.roll(raw, per_row, 1)
        out = []
        for t in range(half):
            first = rows_of[8 * t : 8 * t + 8, :]
            second = rows_of[8 * (own - 1 - t) : 8 * (own - t), :]
            out.append(jnp.where(low, first, pltpu.roll(second, per_row, 1)))
        return out

    for load in loads[:4]:
        load.wait()
    raw_shape = (rows // 2, LANES)
    row_at = lat * rows + 2 * iota(raw_shape, 0) + iota(raw_shape, 1) // per_row
    col_raw = cell_raw[...] - row_at * columns
    weight = weight_raw[...]
    for t, value in enumerate(to_tiles(col_raw)):
        col_tile[t] = value
    for t, value in enumerate(to_tiles(col_raw * 4 + kind_raw[...])):
        key_tile[t] = value
    for t, value in enumerate(to_tiles(weight)):
        wgt_tile[t] = value
    for t, value in enumerate(to_tiles(weight * value_raw[...])):
        wv_tile[t] = value

    los = [col_tile[t] & (LANES - 1) for t in range(half)]
    his = [lax.shift_right_logical(col_tile[t], 7) for t in range(half)]

    def pick(j, accs, tiles):
        out = []
        for t in range(half):
            got = jnp.where(low, lane_gather(tiles[t], los[t]), lane_gather(tiles[own - 1 - t], los[t]))
            out.append(jnp.where(his[t] == j, got, accs[t]))
        return tuple(out)

    def block(j):
        return pl.ds(pl.multiple_of(j * LANES, LANES), LANES)

    zero_tiles = tuple(jnp.zeros(tile, jnp.float32) for _ in range(half))
    loads[4].wait()

    def pick_member(j, accs):
        pairs = [member[16 * k : 16 * k + 16, block(j)].astype(jnp.float32) for k in range(half)]
        tiles = [pair[8 * side : 8 * side + 8] for pair in pairs for side in range(2)]
        return pick(j, accs, tiles)

    for t, value in enumerate(lax.fori_loop(0, blocks, pick_member, zero_tiles)):
        member_at[t] = value

    pl.semaphore_wait(barrier, met + has_up.astype(jnp.int32) + has_down.astype(jnp.int32))

    def halo(index, source, target, device):
        return pltpu.make_async_remote_copy(
            src_ref=source, dst_ref=target, send_sem=halo_send.at[index], recv_sem=halo_recv.at[index],
            device_id=device, device_id_type=MESH,
        )

    sources = (alpha_hbm.at[0], east_hbm, north_hbm)
    targets = (field, east, north)
    to_up = [
        halo(i, s.at[pl.ds(rows - 4, 4)], t.at[pl.ds(rows + 4, 4)], up)
        for i, (s, t) in enumerate(zip(sources, targets))
    ] + [halo(3, col_tile.at[0], col_down, up)]
    to_down = [
        halo(4 + i, s.at[pl.ds(0, 4)], t.at[pl.ds(rows, 4)], down)
        for i, (s, t) in enumerate(zip(sources, targets))
    ] + [halo(7, col_tile.at[0], col_up, down)]

    @pl.when(has_up)
    def _():
        for copy in to_up:
            copy.start()

    @pl.when(has_down)
    def _():
        for copy in to_down:
            copy.start()

    loads[8].wait()

    def pick_back(j, accs):
        return pick(j, accs, [back[8 * t : 8 * t + 8, block(j)] for t in range(own)])

    for t, value in enumerate(lax.fori_loop(0, blocks, pick_back, zero_tiles)):
        back_at[t] = value

    for load in loads[5:8]:
        load.wait()

    @pl.when(has_up)
    def _():
        for copy in to_down:
            copy.wait_recv()

    @pl.when(has_down)
    def _():
        for copy in to_up:
            copy.wait_recv()

    keep = jnp.where((sub >= 4) | has_up, 1.0, 0.0)
    last_lane = lane == LANES - 1
    first_lane = lane == 0
    last_sub = sub == 7
    first_sub = sub == 0
    count = own + 1

    def get(ref, t, j):
        return ref[8 * t : 8 * t + 8, block(j)]

    def diffuse(source, finish, init=()):
        first = [get(source, t, 0) for t in range(count)]
        rolled = tuple(pltpu.roll(v, LANES - 1, 1) for v in first)
        from_west = []
        for t in range(count):
            v = get(source, t, blocks - 1)
            flux = get(east, t, blocks - 1) * (jnp.where(last_lane, rolled[t], pltpu.roll(v, LANES - 1, 1)) - v)
            from_west.append(pltpu.roll(flux, 1, 1))

        def body(j, carry):
            rolled, from_west, extra = carry
            after = lax.rem(j + 1, blocks)
            vs = [get(source, t, j) for t in range(count)]
            lifted = [pltpu.roll(v, 7, 0) for v in vs]
            rise = []
            for t in range(count):
                above = jnp.where(last_sub, lifted[(t + 1) % count], lifted[t])
                rise.append(get(north, t, j) * (above - vs[t]))
            sunk = [pltpu.roll(f, 1, 0) for f in rise]
            next_rolled, next_west, results = [], [], []
            for t in range(count):
                ahead = pltpu.roll(get(source, t, after), LANES - 1, 1)
                flux = get(east, t, j) * (jnp.where(last_lane, ahead, rolled[t]) - vs[t])
                turned = pltpu.roll(flux, 1, 1)
                west = jnp.where(first_lane, from_west[t], turned)
                south = jnp.where(first_sub, sunk[t - 1], sunk[t])
                result = vs[t] + ((flux - west) + (rise[t] - south))
                results.append(result * keep if t == own else result)
                next_rolled.append(ahead)
                next_west.append(turned)
            return tuple(next_rolled), tuple(next_west), finish(j, results, extra)

        return lax.fori_loop(0, blocks, body, (rolled, tuple(from_west), init))[2]

    def into(target):
        def finish(j, results, extra):
            for t in range(count):
                target[8 * t : 8 * t + 8, block(j)] = results[t]
            return extra

        return finish

    diffuse(field, into(ping))
    diffuse(ping, into(pong))
    diffuse(pong, into(ping))
    picked = diffuse(ping, lambda j, results, accs: pick(j, accs, results), zero_tiles)
    for t in range(half):
        part[t] = member_at[t] * picked[t]

    def stage_copy(t, stage, index, ahead, slot):
        name = ORDERS[t % len(ORDERS)][stage]
        return pltpu.make_async_remote_copy(
            src_ref=part.at[stage * half + t], dst_ref=inbox.at[slot],
            send_sem=stage_send.at[slot], recv_sem=stage_recv.at[slot],
            device_id=peer(name, ahead), device_id_type=MESH,
        )

    copies = []
    slot = 0
    for t in range(half):
        of_tile = []
        for stage in range(3):
            of_stage = []
            for ahead in range(1, sizes[ORDERS[t % len(ORDERS)][stage]]):
                of_stage.append((stage_copy(t, stage, 0, ahead, slot), slot))
                slot += 1
            of_tile.append(of_stage)
        copies.append(of_tile)

    def send(t, stage):
        for copy, _ in copies[t][stage]:
            copy.start()

    def collect(t, stage):
        total = part[stage * half + t]
        for copy, at in copies[t][stage]:
            copy.wait_recv()
            total = total + inbox[at]
        return total

    for t in range(half):
        send(t, 0)

    half_base = lane & per_row
    in_half = lane & (per_row - 1)
    for t in range(half):
        key = key_tile[t]
        col = col_tile[t]
        wgt = wgt_tile[t]
        wv = wv_tile[t]
        kind = key & 3

        def merge(d, carry, col=col, key=key, wgt=wgt, wv=wv):
            w0, w1, w2, v0, v1, v2, repeat = carry
            lanes = half_base | ((lane - d) & (per_row - 1))
            other = lane_gather(key, lanes)
            w = lane_gather(wgt, lanes)
            v = lane_gather(wv, lanes)
            same = lax.shift_right_logical(other, 2) == col
            kind = other & 3
            m0 = same & (kind == 0)
            m1 = same & (kind == 1)
            m2 = same & (kind == 2)
            return (
                w0 + jnp.where(m0, w, 0.0), w1 + jnp.where(m1, w, 0.0), w2 + jnp.where(m2, w, 0.0),
                v0 + jnp.where(m0, v, 0.0), v1 + jnp.where(m1, v, 0.0), v2 + jnp.where(m2, v, 0.0),
                jnp.where(same & (in_half >= d), 1, repeat),
            )

        init = tuple(jnp.where(kind == k, wgt, 0.0) for k in range(3)) + tuple(
            jnp.where(kind == k, wv, 0.0) for k in range(3)
        ) + (jnp.zeros(tile, jnp.int32),)
        merged = lax.fori_loop(1, per_row, merge, init)
        for k in range(6):
            sums[6 * t + k] = merged[k]
        rep_tile[t] = jnp.where(merged[6] == 0, lane + 1, 0)

    for t in range(half):
        total = collect(t, 0)
        part[half + t] = total
        send(t, 1)

    halo_cols = jnp.where(sub < 4, col_up[...], col_down[...])
    col_tile[half] = halo_cols

    def find_repeat(d, repeat):
        lanes = half_base | ((lane - d) & (per_row - 1))
        return jnp.where((lane_gather(halo_cols, lanes) == halo_cols) & (in_half >= d), 1, repeat)

    repeat = lax.fori_loop(1, per_row, find_repeat, jnp.zeros(tile, jnp.int32))
    rep_tile[half] = jnp.where(repeat == 0, lane + 1, 0)

    def spot(t, s):
        col = col_tile[t, pl.ds(s, 1), :]
        rep = rep_tile[t, pl.ds(s, 1), :].astype(jnp.float32)
        hi = lax.shift_right_logical(col, 7)
        lo = col & (LANES - 1)
        ones = jnp.where(iota((LANES, LANES), 0) == lo, 1.0, 0.0).astype(jnp.bfloat16)
        at = jnp.where(iota((blocks, LANES), 0) == hi, rep, 0.0)
        right = iota((blocks, LANES), 1) < per_row
        split = jnp.concatenate([jnp.where(right, at, 0.0), jnp.where(right, 0.0, at)], axis=0).astype(jnp.bfloat16)
        return lax.dot_general(split, ones, (((1,), (1,)), ((), ())), preferred_element_type=jnp.float32)

    def own_rows(s, carry):
        for t in range(half):
            found = spot(t, s)
            inverse[t, pl.ds(s, blocks, stride=8), :] = found[:blocks]
            inverse[own - 1 - t, pl.ds(s, blocks, stride=8), :] = found[blocks:]
        return carry

    lax.fori_loop(0, 8, own_rows, 0)

    def halo_rows(s, carry):
        found = spot(half, s)
        inverse[own, pl.ds(s, blocks, stride=8), :] = jnp.where(s < 4, found[:blocks], found[blocks:])
        return carry

    lax.fori_loop(0, 8, halo_rows, 0)

    for t in range(half):
        total = collect(t, 1)
        part[2 * half + t] = total
        send(t, 2)

    uses = []
    for t in range(half):
        s = back_at[t] + collect(t, 2)
        w0, w1, w2, v0, v1, v2 = [sums[6 * t + k] for k in range(6)]
        size = jnp.abs(s)
        small = jnp.exp(-2.0 * size)
        soft = jnp.maximum(2.0 * s, 0.0) + jnp.log1p(small)
        slope = jnp.where(s >= 0, 1.0, small) / (1.0 + small)
        misfit = (w0 * s - v0) + (w1 * (0.5 * s * size) - v1) * size + (w2 * (0.5 * soft) - v2) * slope
        use = member_at[t] * misfit
        uses.append(use)
        use_tile[t] = use
        if t == 0:
            use_to_up = halo(8, use_tile.at[0], use_down, up)
            use_to_down = halo(9, use_tile.at[0], use_up, down)

            @pl.when(has_up)
            def _():
                use_to_up.start()

            @pl.when(has_down)
            def _():
                use_to_down.start()

    def place_tile(t, values):
        for j in range(blocks):
            found = inverse[t, 8 * j : 8 * j + 8, :].astype(jnp.int32)
            got = lane_gather(values, jnp.maximum(found - 1, 0))
            ping[8 * t : 8 * t + 8, j * LANES : (j + 1) * LANES] = jnp.where(found > 0, got, 0.0)

    for t in range(half):
        place_tile(t, uses[t])
        place_tile(own - 1 - t, uses[t])

    @pl.when(has_up)
    def _():
        use_to_down.wait_recv()

    @pl.when(has_down)
    def _():
        use_to_up.wait_recv()

    place_tile(own, jnp.where(sub < 4, use_up[...], use_down[...]))

    def to_out(j, results, extra):
        for t in range(own):
            out_ref[0, 8 * t : 8 * t + 8, block(j)] = results[t] + get(field, t, j)
        return extra

    diffuse(ping, into(pong))
    diffuse(pong, into(ping))
    diffuse(ping, into(pong))
    diffuse(pong, to_out)

    for of_tile in copies:
        for of_stage in of_tile:
            for copy, _ in of_stage:
                copy.wait_send()

    @pl.when(has_up)
    def _():
        for copy in to_up + [use_to_up]:
            copy.wait_send()

    @pl.when(has_down)
    def _():
        for copy in to_down + [use_to_down]:
            copy.wait_send()


def make(mesh, axes=AXES):
    def per_device(ensemble, alpha, background, east_coef, north_coef, obs_cell, obs_type, obs_value, obs_weight):
        rows, columns = background.shape
        blocks = columns // LANES
        own = rows // 8
        half = own // 2
        ext = rows + 8
        packed = (rows // 2, LANES)
        tile = (8, LANES)
        slots = half * sum(size - 1 for _, size in axes)
        f32, i32 = jnp.float32, jnp.int32
        VMEM = pltpu.VMEM
        scratch = [
            VMEM((ext, columns), f32), VMEM((ext, columns), f32), VMEM((ext, columns), f32),
            VMEM((ext, columns), f32), VMEM((ext, columns), f32),
            VMEM((rows, columns), jnp.bfloat16), VMEM((rows, columns), f32),
            VMEM(packed, i32), VMEM(packed, i32), VMEM(packed, f32), VMEM(packed, f32),
            VMEM((rows, LANES), i32), VMEM((rows, LANES), f32),
            VMEM((half + 1, *tile), i32), VMEM((half, *tile), i32), VMEM((half, *tile), f32), VMEM((half, *tile), f32),
            VMEM((6 * half, *tile), f32), VMEM((half, *tile), f32), VMEM((half, *tile), f32),
            VMEM((half + 1, *tile), i32), VMEM((own + 1, 8 * blocks, LANES), f32),
            VMEM(tile, i32), VMEM(tile, i32), VMEM((half, *tile), f32), VMEM(tile, f32), VMEM(tile, f32),
            VMEM((3 * half, *tile), f32), VMEM((slots, *tile), f32),
            pltpu.SemaphoreType.DMA((9,)), pltpu.SemaphoreType.DMA((10,)), pltpu.SemaphoreType.DMA((10,)),
            pltpu.SemaphoreType.DMA((slots,)), pltpu.SemaphoreType.DMA((slots,)),
        ]
        return pl.pallas_call(
            functools.partial(kernel, axes),
            out_shape=jax.ShapeDtypeStruct((1, rows, columns), f32),
            in_specs=[pl.BlockSpec(memory_space=pl.ANY)] * 9,
            out_specs=pl.BlockSpec(memory_space=pltpu.VMEM),
            scratch_shapes=scratch,
            compiler_params=pltpu.CompilerParams(collective_id=0, has_side_effects=True),
            name="gradient",
        )(
            alpha, ensemble, background, east_coef, north_coef,
            obs_cell.reshape(packed), obs_type.reshape(packed), obs_value.reshape(packed), obs_weight.reshape(packed),
        )

    return jax.shard_map(
        per_device,
        mesh=mesh,
        in_specs=(
            P("mem", "lat", None), P("mem", "lat", None), P("lat", None), P("lat", None), P("lat", None),
            P("lat"), P("lat"), P("lat"), P("lat"),
        ),
        out_specs=P("mem", "lat", None),
        check_vma=False,
    )


def solution(mesh):
    return make(mesh)
```

```python
import functools
import itertools

import jax
import jax.numpy as jnp
from jax import lax
from jax.experimental import pallas as pl
from jax.experimental.pallas import tpu as pltpu
from jax.sharding import PartitionSpec as P

PASSES = 4
AXES = (("y", 2), ("x", 4), ("z", 8))
ORDERS = (("z", "xy"), ("xy", "z"), ("z", "xy"), ("xy", "z"))
HOPS = {"y": 4, "x": 1, "z": 1}
LANES = 128
UNROLL = 24
LIMIT = 20 * 2**20
MESH = pl.DeviceIdType.MESH


def iota(shape, dim):
    return lax.broadcasted_iota(jnp.int32, shape, dim)


def lane_gather(values, lanes):
    return jnp.take_along_axis(values, lanes, axis=1, mode="promise_in_bounds")


def kernel(
    axes, alpha_hbm, member_hbm, back_hbm, east_hbm, north_hbm, cell_hbm, kind_hbm, value_hbm, weight_hbm,
    out_ref,
    field, east, north, ping, pong, third, edge_a, edge_b, member, back,
    cell_raw, kind_raw, value_raw, weight_raw, rows_int, rows_float,
    col_tile, key_tile, wgt_tile, wv_tile, sums, member_at, back_at, rep_tile, inverse,
    col_up, col_down, use_tile, use_up, use_down, part, inbox,
    load_sem, halo_send, halo_recv, stage_send, stage_recv, relay,
):
    rows = alpha_hbm.shape[1]
    columns = alpha_hbm.shape[2]
    blocks = columns // LANES
    own = rows // 8
    half = own // 2
    unroll = UNROLL if blocks % UNROLL == 0 else 1
    per_row = LANES // 2
    lat = lax.axis_index("lat")
    lats = lax.axis_size("lat")
    mem = lax.axis_index("mem")
    has_up = lat < lats - 1
    has_down = lat > 0

    place = {}
    stride = {}
    rest = mem
    step = 1
    for name, size in reversed(axes):
        place[name] = lax.rem(rest, size)
        stride[name] = step
        rest = rest // size
        step = step * size
    sizes = dict(axes)

    def peer(move):
        to = mem
        for name, ahead in move:
            there = lax.rem(place[name] + ahead, sizes[name])
            to = to + (there - place[name]) * stride[name]
        return {"mem": to, "lat": lat}

    def hops(move):
        return sum(HOPS[name] * min(ahead, sizes[name] - ahead) for name, ahead in move)

    def moves(names):
        every = itertools.product(*[[(name, ahead) for ahead in range(sizes[name])] for name in names])
        return sorted((m for m in every if any(ahead for _, ahead in m)), key=hops, reverse=True)

    up = {"mem": mem, "lat": lat + 1}
    down = {"mem": mem, "lat": lat - 1}

    barrier = pltpu.get_barrier_semaphore()
    met = 0
    for name, size in axes:
        for move in moves(name):
            pl.semaphore_signal(barrier, inc=1, device_id=peer(move), device_id_type=MESH)
            met += 1

    @pl.when(has_up)
    def _():
        pl.semaphore_signal(barrier, inc=1, device_id=up, device_id_type=MESH)

    @pl.when(has_down)
    def _():
        pl.semaphore_signal(barrier, inc=1, device_id=down, device_id_type=MESH)

    loads = [
        pltpu.make_async_copy(source, target, load_sem.at[index])
        for index, (source, target) in enumerate((
            (cell_hbm, cell_raw), (kind_hbm, kind_raw), (value_hbm, value_raw), (weight_hbm, weight_raw),
            (member_hbm.at[0], member), (alpha_hbm.at[0], field.at[pl.ds(0, rows)]),
            (east_hbm, east.at[pl.ds(0, rows)]), (north_hbm, north.at[pl.ds(0, rows)]), (back_hbm, back),
        ))
    ]
    for load in loads:
        load.start()

    tile = (8, LANES)
    lane = iota(tile, 1)
    sub = iota(tile, 0)
    low = lane < per_row

    zeros4 = jnp.zeros((4, columns), jnp.float32)

    @pl.when(jnp.logical_not(has_up))
    def _():
        for ref in (field, east, north):
            ref[rows : rows + 4, :] = zeros4
        col_up[...] = jnp.zeros(tile, jnp.int32)
        use_up[...] = jnp.zeros(tile, jnp.float32)

    @pl.when(jnp.logical_not(has_down))
    def _():
        for ref in (field, east, north):
            ref[rows + 4 : rows + 8, :] = zeros4
        col_down[...] = jnp.zeros(tile, jnp.int32)
        use_down[...] = jnp.zeros(tile, jnp.float32)

    def to_tiles(raw):
        rows_of = rows_int if raw.dtype == jnp.int32 else rows_float
        rows_of[pl.ds(0, rows // 2, stride=2), :] = raw
        rows_of[pl.ds(1, rows // 2, stride=2), :] = pltpu.roll(raw, per_row, 1)
        out = []
        for t in range(half):
            first = rows_of[8 * t : 8 * t + 8, :]
            second = rows_of[8 * (own - 1 - t) : 8 * (own - t), :]
            out.append(jnp.where(low, first, pltpu.roll(second, per_row, 1)))
        return out

    for load in loads[:4]:
        load.wait()
    raw_shape = (rows // 2, LANES)
    row_at = lat * rows + 2 * iota(raw_shape, 0) + iota(raw_shape, 1) // per_row
    col_raw = cell_raw[...] - row_at * columns
    weight = weight_raw[...]
    for t, value in enumerate(to_tiles(col_raw)):
        col_tile[t] = value
    for t, value in enumerate(to_tiles(col_raw * 4 + kind_raw[...])):
        key_tile[t] = value
    for t, value in enumerate(to_tiles(weight)):
        wgt_tile[t] = value
    for t, value in enumerate(to_tiles(weight * value_raw[...])):
        wv_tile[t] = value

    los = [col_tile[t] & (LANES - 1) for t in range(half)]
    his = [lax.shift_right_logical(col_tile[t], 7) for t in range(half)]

    def pick(j, accs, tiles):
        out = []
        for t in range(half):
            got = jnp.where(low, lane_gather(tiles[t], los[t]), lane_gather(tiles[own - 1 - t], los[t]))
            out.append(jnp.where(his[t] == j, got, accs[t]))
        return tuple(out)

    def block(j):
        return pl.ds(pl.multiple_of(j * LANES, LANES), LANES)

    zero_tiles = tuple(jnp.zeros(tile, jnp.float32) for _ in range(half))

    def over_blocks(step):
        def body(i, accs):
            for u in range(unroll):
                accs = step(i * unroll + u, accs)
            return accs

        return lax.fori_loop(0, blocks // unroll, body, zero_tiles)

    loads[4].wait()

    def pick_member(j, accs):
        pairs = [member[16 * k : 16 * k + 16, block(j)].astype(jnp.float32) for k in range(half)]
        tiles = [pair[8 * side : 8 * side + 8] for pair in pairs for side in range(2)]
        return pick(j, accs, tiles)

    for t, value in enumerate(over_blocks(pick_member)):
        member_at[t] = value

    pl.semaphore_wait(barrier, met + has_up.astype(jnp.int32) + has_down.astype(jnp.int32))

    for move in moves("x"):
        pl.semaphore_signal(relay, inc=1, device_id=peer(move), device_id_type=MESH)

    def halo(index, source, target, device):
        return pltpu.make_async_remote_copy(
            src_ref=source, dst_ref=target, send_sem=halo_send.at[index], recv_sem=halo_recv.at[index],
            device_id=device, device_id_type=MESH,
        )

    sources = (alpha_hbm.at[0], east_hbm, north_hbm)
    targets = (field, east, north)
    to_up = [
        halo(i, s.at[pl.ds(rows - 4, 4)], t.at[pl.ds(rows + 4, 4)], up)
        for i, (s, t) in enumerate(zip(sources, targets))
    ] + [halo(3, col_tile.at[0], col_down, up)]
    to_down = [
        halo(4 + i, s.at[pl.ds(0, 4)], t.at[pl.ds(rows, 4)], down)
        for i, (s, t) in enumerate(zip(sources, targets))
    ] + [halo(7, col_tile.at[0], col_up, down)]

    @pl.when(has_up)
    def _():
        for copy in to_up:
            copy.start()

    @pl.when(has_down)
    def _():
        for copy in to_down:
            copy.start()

    for load in loads[5:8]:
        load.wait()

    keep = jnp.where((sub >= 4) | has_up, 1.0, 0.0)
    last_lane = lane == LANES - 1
    first_lane = lane == 0
    last_sub = sub == 7
    first_sub = sub == 0
    def get(ref, t, j):
        return ref[8 * t : 8 * t + 8, block(j)]

    def diffuse(source, tiles, coefs, finish, init=()):
        turn = LANES - 1
        ring = range(len(tiles))
        rolled = tuple(pltpu.roll(get(source, t, 0), turn, 1) for t in tiles)
        from_west = []
        for k in ring:
            v = get(source, tiles[k], blocks - 1)
            flux = get(east, coefs[k], blocks - 1) * (jnp.where(last_lane, rolled[k], pltpu.roll(v, turn, 1)) - v)
            from_west.append(pltpu.roll(flux, 1, 1))

        def body(i, carry):
            rolled, from_west, extra = carry
            for u in range(unroll):
                j = i * unroll + u
                after = j + 1
                if u == unroll - 1:
                    after = jnp.where(after == blocks, 0, after)
                vs = [get(source, t, j) for t in tiles]
                lifted = [pltpu.roll(v, 7, 0) for v in vs]
                rise = []
                for k in ring:
                    above = jnp.where(last_sub, lifted[(k + 1) % len(tiles)], lifted[k])
                    rise.append(get(north, coefs[k], j) * (above - vs[k]))
                sunk = [pltpu.roll(f, 1, 0) for f in rise]
                next_rolled, next_west, results = [], [], []
                for k in ring:
                    ahead = pltpu.roll(get(source, tiles[k], after), turn, 1)
                    flux = get(east, coefs[k], j) * (jnp.where(last_lane, ahead, rolled[k]) - vs[k])
                    turned = pltpu.roll(flux, 1, 1)
                    west = jnp.where(first_lane, from_west[k], turned)
                    south = jnp.where(first_sub, sunk[k - 1], sunk[k])
                    result = vs[k] + ((flux - west) + (rise[k] - south))
                    results.append(result * keep if coefs[k] == own else result)
                    next_rolled.append(ahead)
                    next_west.append(turned)
                rolled, from_west = tuple(next_rolled), tuple(next_west)
                extra = finish(j, results, extra)
            return rolled, from_west, extra

        return lax.fori_loop(0, blocks // unroll, body, (rolled, tuple(from_west), init))[2]

    def into(target):
        def finish(j, results, extra):
            for t, result in enumerate(results):
                target[8 * t : 8 * t + 8, block(j)] = result
            return extra

        return finish

    inner = list(range(own))
    edge = [own - 1, own, 0]
    flat = [0, 1, 2]
    from_edge = jnp.where(low, sub, 7 - sub) < 4

    diffuse(field, inner, inner, into(ping))
    diffuse(ping, inner, inner, into(pong))
    diffuse(pong, inner, inner, into(ping))
    picked = diffuse(ping, inner, inner, lambda j, results, accs: pick(j, accs, results), zero_tiles)
    for t in range(1, half):
        part[t] = member_at[t] * picked[t]

    def stage_copy(t, stage, move, slot):
        return pltpu.make_async_remote_copy(
            src_ref=part.at[stage * half + t], dst_ref=inbox.at[slot],
            send_sem=stage_send.at[slot], recv_sem=stage_recv.at[slot],
            device_id=peer(move), device_id_type=MESH,
        )

    copies = []
    slot = 0
    for t in range(half):
        of_tile = []
        for stage in range(2):
            of_stage = []
            for move in moves(ORDERS[t % len(ORDERS)][stage]):
                of_stage.append((stage_copy(t, stage, move, slot), slot))
                slot += 1
            of_tile.append(of_stage)
        copies.append(of_tile)

    def send(t, stage):
        for copy, _ in copies[t][stage]:
            copy.start()

    def collect(t, stage):
        total = part[stage * half + t]
        for copy, at in copies[t][stage]:
            copy.wait_recv()
            total = total + inbox[at]
        return total

    pl.semaphore_wait(relay, len(moves("x")))
    for t in range(1, half):
        send(t, 0)

    @pl.when(has_up)
    def _():
        for copy in to_down:
            copy.wait_recv()

    @pl.when(has_down)
    def _():
        for copy in to_up:
            copy.wait_recv()

    def pick_edge(j, results, acc):
        got = jnp.where(low, lane_gather(results[2], los[0]), lane_gather(results[0], los[0]))
        return jnp.where(his[0] == j, got, acc)

    diffuse(field, edge, edge, into(edge_a))
    diffuse(edge_a, flat, edge, into(edge_b))
    diffuse(edge_b, flat, edge, into(edge_a))
    picked_edge = diffuse(edge_a, flat, edge, pick_edge, zero_tiles[0])
    part[0] = member_at[0] * jnp.where(from_edge, picked_edge, picked[0])
    send(0, 0)

    half_base = lane & per_row
    in_half = lane & (per_row - 1)

    def merge(i, carry):
        carry = list(carry)
        for u in range(3):
            d = 3 * i + 1 + u
            lanes = half_base | ((lane - d) & (per_row - 1))
            later = in_half >= d
            for t in range(half):
                w0, w1, w2, v0, v1, v2, repeat = carry[t]
                other = lane_gather(key_tile[t], lanes)
                w = lane_gather(wgt_tile[t], lanes)
                v = lane_gather(wv_tile[t], lanes)
                same = lax.shift_right_logical(other, 2) == col_tile[t]
                kind = other & 3
                m0 = same & (kind == 0)
                m1 = same & (kind == 1)
                m2 = same & (kind == 2)
                carry[t] = (
                    w0 + jnp.where(m0, w, 0.0), w1 + jnp.where(m1, w, 0.0), w2 + jnp.where(m2, w, 0.0),
                    v0 + jnp.where(m0, v, 0.0), v1 + jnp.where(m1, v, 0.0), v2 + jnp.where(m2, v, 0.0),
                    jnp.where(same & later, 1, repeat),
                )
        return tuple(carry)

    start = []
    for t in range(half):
        kind = key_tile[t] & 3
        start.append(
            tuple(jnp.where(kind == k, wgt_tile[t], 0.0) for k in range(3))
            + tuple(jnp.where(kind == k, wv_tile[t], 0.0) for k in range(3))
            + (jnp.zeros(tile, jnp.int32),)
        )
    merged = lax.fori_loop(0, (per_row - 1) // 3, merge, tuple(start))
    for t in range(half):
        for k in range(6):
            sums[6 * t + k] = merged[t][k]
        rep_tile[t] = jnp.where(merged[t][6] == 0, lane + 1, 0)

    loads[8].wait()

    def pick_back(j, accs):
        return pick(j, accs, [back[8 * t : 8 * t + 8, block(j)] for t in range(own)])

    for t, value in enumerate(over_blocks(pick_back)):
        back_at[t] = value

    for t in range(1, half):
        total = collect(t, 0)
        part[half + t] = total
        send(t, 1)

    halo_cols = jnp.where(sub < 4, col_up[...], col_down[...])
    col_tile[half] = halo_cols

    def find_repeat(i, repeat):
        for u in range(9):
            d = 9 * i + 1 + u
            lanes = half_base | ((lane - d) & (per_row - 1))
            repeat = jnp.where((lane_gather(halo_cols, lanes) == halo_cols) & (in_half >= d), 1, repeat)
        return repeat

    repeat = lax.fori_loop(0, (per_row - 1) // 9, find_repeat, jnp.zeros(tile, jnp.int32))
    rep_tile[half] = jnp.where(repeat == 0, lane + 1, 0)

    def spot(t, s):
        col = col_tile[t, pl.ds(s, 1), :]
        rep = rep_tile[t, pl.ds(s, 1), :].astype(jnp.float32)
        hi = lax.shift_right_logical(col, 7)
        lo = col & (LANES - 1)
        ones = jnp.where(iota((LANES, LANES), 0) == lo, 1.0, 0.0).astype(jnp.bfloat16)
        at = jnp.where(iota((blocks, LANES), 0) == hi, rep, 0.0)
        right = iota((blocks, LANES), 1) < per_row
        split = jnp.concatenate([jnp.where(right, at, 0.0), jnp.where(right, 0.0, at)], axis=0).astype(jnp.bfloat16)
        return lax.dot_general(split, ones, (((1,), (1,)), ((), ())), preferred_element_type=jnp.float32)

    def all_rows(i, carry):
        for s in (2 * i, 2 * i + 1):
            for t in range(half):
                found = spot(t, s)
                inverse[t, pl.ds(s, blocks, stride=8), :] = found[:blocks]
                inverse[own - 1 - t, pl.ds(s, blocks, stride=8), :] = found[blocks:]
            found = spot(half, s)
            inverse[own, pl.ds(s, blocks, stride=8), :] = jnp.where(s < 4, found[:blocks], found[blocks:])
        return carry

    lax.fori_loop(0, 4, all_rows, 0)

    part[half] = collect(0, 0)
    send(0, 1)

    def use_of(t):
        s = back_at[t] + collect(t, 1)
        w0, w1, w2, v0, v1, v2 = [sums[6 * t + k] for k in range(6)]
        size = jnp.abs(s)
        small = jnp.exp(-2.0 * size)
        soft = jnp.maximum(2.0 * s, 0.0) + jnp.log1p(small)
        slope = jnp.where(s >= 0, 1.0, small) / (1.0 + small)
        misfit = (w0 * s - v0) + (w1 * (0.5 * s * size) - v1) * size + (w2 * (0.5 * soft) - v2) * slope
        return member_at[t] * misfit

    def place_tile(t, values):
        for j in range(blocks):
            found = inverse[t, 8 * j : 8 * j + 8, :].astype(jnp.int32)
            got = lane_gather(values, jnp.maximum(found - 1, 0))
            ping[8 * t : 8 * t + 8, j * LANES : (j + 1) * LANES] = jnp.where(found > 0, got, 0.0)

    for t in range(1, half):
        use = use_of(t)
        place_tile(t, use)
        place_tile(own - 1 - t, use)

    use = use_of(0)
    use_tile[0] = use
    use_to_up = halo(8, use_tile.at[0], use_down, up)
    use_to_down = halo(9, use_tile.at[0], use_up, down)

    @pl.when(has_up)
    def _():
        use_to_up.start()

    @pl.when(has_down)
    def _():
        use_to_down.start()

    place_tile(0, use)
    place_tile(own - 1, use)

    def to_out(j, results, extra):
        for t in range(own):
            out_ref[0, 8 * t : 8 * t + 8, block(j)] = results[t] + get(field, t, j)
        return extra

    def edge_out(j, results, extra):
        for k, t, mine in ((2, 0, sub < 4), (0, own - 1, sub >= 4)):
            rows_at = pl.ds(8 * t, 8)
            value = jnp.where(mine, results[k] + get(field, t, j), out_ref[0, rows_at, block(j)])
            out_ref[0, rows_at, block(j)] = value
        return extra

    diffuse(ping, inner, inner, into(pong))
    diffuse(pong, inner, inner, into(third))
    diffuse(third, inner, inner, into(pong))
    diffuse(pong, inner, inner, to_out)

    @pl.when(has_up)
    def _():
        use_to_down.wait_recv()

    @pl.when(has_down)
    def _():
        use_to_up.wait_recv()

    place_tile(own, jnp.where(sub < 4, use_up[...], use_down[...]))
    diffuse(ping, edge, edge, into(edge_a))
    diffuse(edge_a, flat, edge, into(edge_b))
    diffuse(edge_b, flat, edge, into(edge_a))
    diffuse(edge_a, flat, edge, edge_out)

    for of_tile in copies:
        for of_stage in of_tile:
            for copy, _ in of_stage:
                copy.wait_send()

    @pl.when(has_up)
    def _():
        for copy in to_up + [use_to_up]:
            copy.wait_send()

    @pl.when(has_down)
    def _():
        for copy in to_down + [use_to_down]:
            copy.wait_send()


def make(mesh, axes=AXES):
    def per_device(ensemble, alpha, background, east_coef, north_coef, obs_cell, obs_type, obs_value, obs_weight):
        rows, columns = background.shape
        blocks = columns // LANES
        own = rows // 8
        half = own // 2
        ext = rows + 8
        packed = (rows // 2, LANES)
        tile = (8, LANES)
        count = dict(axes)
        slots = half * (count["x"] * count["y"] + count["z"] - 2)
        f32, i32 = jnp.float32, jnp.int32
        VMEM = pltpu.VMEM
        scratch = [
            VMEM((ext, columns), f32), VMEM((ext, columns), f32), VMEM((ext, columns), f32),
            VMEM((ext, columns), f32), VMEM((ext, columns), f32), VMEM((rows, columns), f32),
            VMEM((24, columns), f32), VMEM((24, columns), f32),
            VMEM((rows, columns), jnp.bfloat16), VMEM((rows, columns), f32),
            VMEM(packed, i32), VMEM(packed, i32), VMEM(packed, f32), VMEM(packed, f32),
            VMEM((rows, LANES), i32), VMEM((rows, LANES), f32),
            VMEM((half + 1, *tile), i32), VMEM((half, *tile), i32), VMEM((half, *tile), f32), VMEM((half, *tile), f32),
            VMEM((6 * half, *tile), f32), VMEM((half, *tile), f32), VMEM((half, *tile), f32),
            VMEM((half + 1, *tile), i32), VMEM((own + 1, 8 * blocks, LANES), f32),
            VMEM(tile, i32), VMEM(tile, i32), VMEM((half, *tile), f32), VMEM(tile, f32), VMEM(tile, f32),
            VMEM((2 * half, *tile), f32), VMEM((slots, *tile), f32),
            pltpu.SemaphoreType.DMA((9,)), pltpu.SemaphoreType.DMA((10,)), pltpu.SemaphoreType.DMA((10,)),
            pltpu.SemaphoreType.DMA((slots,)), pltpu.SemaphoreType.DMA((slots,)), pltpu.SemaphoreType.REGULAR,
        ]
        return pl.pallas_call(
            functools.partial(kernel, axes),
            out_shape=jax.ShapeDtypeStruct((1, rows, columns), f32),
            in_specs=[pl.BlockSpec(memory_space=pltpu.HBM)] * 9,
            out_specs=pl.BlockSpec(memory_space=pltpu.VMEM),
            scratch_shapes=scratch,
            compiler_params=pltpu.CompilerParams(collective_id=0, has_side_effects=True, vmem_limit_bytes=LIMIT),
            name="gradient",
        )(*[pltpu.with_memory_space_constraint(a, pltpu.HBM) for a in (
            alpha, ensemble, background, east_coef, north_coef,
            obs_cell.reshape(packed), obs_type.reshape(packed), obs_value.reshape(packed), obs_weight.reshape(packed),
        )])

    return jax.shard_map(
        per_device,
        mesh=mesh,
        in_specs=(
            P("mem", "lat", None), P("mem", "lat", None), P("lat", None), P("lat", None), P("lat", None),
            P("lat"), P("lat"), P("lat"), P("lat"),
        ),
        out_specs=P("mem", "lat", None),
        check_vma=False,
    )


def solution(mesh):
    return make(mesh)
```

```python
import functools
import itertools

import jax
import jax.numpy as jnp
from jax import lax
from jax.experimental import pallas as pl
from jax.experimental.pallas import tpu as pltpu
from jax.sharding import PartitionSpec as P

PASSES = 4
AXES = (("y", 2), ("x", 4), ("z", 8))
ORDERS = (("z", "xy"), ("xy", "z"), ("z", "xy"), ("xy", "z"))
HOPS = {"y": 4, "x": 1, "z": 1}
LANES = 128
LIMIT = 20 * 2**20
MESH = pl.DeviceIdType.MESH


def iota(shape, dim):
    return lax.broadcasted_iota(jnp.int32, shape, dim)


def lane_gather(values, lanes):
    return jnp.take_along_axis(values, lanes, axis=1, mode="promise_in_bounds")


def kernel(
    axes, alpha_hbm, member_hbm, back_hbm, east_hbm, north_hbm, cell_hbm, kind_hbm, value_hbm, weight_hbm,
    out_ref,
    field, east, north, west, ping, pong, third, edge_a, edge_b, member, back,
    cell_raw, kind_raw, value_raw, weight_raw, rows_int, rows_float,
    col_tile, key_tile, wgt_tile, wv_tile, sums, member_at, back_at, rep_tile, inverse,
    col_up, col_down, use_tile, use_up, use_down, part, inbox,
    load_sem, halo_send, halo_recv, stage_send, stage_recv, relay,
):
    rows = alpha_hbm.shape[1]
    columns = alpha_hbm.shape[2]
    blocks = columns // LANES
    own = rows // 8
    half = own // 2
    per_row = LANES // 2
    loads = [
        pltpu.make_async_copy(source, target, load_sem.at[index])
        for index, (source, target) in enumerate((
            (alpha_hbm.at[0], field.at[pl.ds(0, rows)]), (east_hbm, east.at[pl.ds(0, rows)]),
            (north_hbm, north.at[pl.ds(0, rows)]), (cell_hbm, cell_raw), (kind_hbm, kind_raw),
            (value_hbm, value_raw), (weight_hbm, weight_raw), (member_hbm.at[0], member), (back_hbm, back),
        ))
    ]
    for load in loads:
        load.start()

    lat = lax.axis_index("lat")
    lats = lax.axis_size("lat")
    mem = lax.axis_index("mem")
    has_up = lat < lats - 1
    has_down = lat > 0

    place = {}
    stride = {}
    rest = mem
    step = 1
    for name, size in reversed(axes):
        place[name] = lax.rem(rest, size)
        stride[name] = step
        rest = rest // size
        step = step * size
    sizes = dict(axes)

    def peer(move):
        to = mem
        for name, ahead in move:
            there = lax.rem(place[name] + ahead, sizes[name])
            to = to + (there - place[name]) * stride[name]
        return {"mem": to, "lat": lat}

    def hops(move):
        return sum(HOPS[name] * min(ahead, sizes[name] - ahead) for name, ahead in move)

    def moves(names):
        every = itertools.product(*[[(name, ahead) for ahead in range(sizes[name])] for name in names])
        return sorted((m for m in every if any(ahead for _, ahead in m)), key=hops, reverse=True)

    up = {"mem": mem, "lat": lat + 1}
    down = {"mem": mem, "lat": lat - 1}

    barrier = pltpu.get_barrier_semaphore()
    met = 0
    for name, size in axes:
        for move in moves(name):
            pl.semaphore_signal(barrier, inc=1, device_id=peer(move), device_id_type=MESH)
            met += 1

    @pl.when(has_up)
    def _():
        pl.semaphore_signal(barrier, inc=1, device_id=up, device_id_type=MESH)

    @pl.when(has_down)
    def _():
        pl.semaphore_signal(barrier, inc=1, device_id=down, device_id_type=MESH)

    pl.semaphore_wait(barrier, met + has_up.astype(jnp.int32) + has_down.astype(jnp.int32))

    for move in moves("x"):
        pl.semaphore_signal(relay, inc=1, device_id=peer(move), device_id_type=MESH)

    def halo(index, source, target, device):
        return pltpu.make_async_remote_copy(
            src_ref=source, dst_ref=target, send_sem=halo_send.at[index], recv_sem=halo_recv.at[index],
            device_id=device, device_id_type=MESH,
        )

    sources = (alpha_hbm.at[0], east_hbm, north_hbm)
    targets = (field, east, north)
    to_up = [
        halo(i, s.at[pl.ds(rows - 4, 4)], t.at[pl.ds(rows + 4, 4)], up)
        for i, (s, t) in enumerate(zip(sources, targets))
    ]
    to_down = [
        halo(4 + i, s.at[pl.ds(0, 4)], t.at[pl.ds(rows, 4)], down)
        for i, (s, t) in enumerate(zip(sources, targets))
    ]

    @pl.when(has_up)
    def _():
        for copy in to_up:
            copy.start()

    @pl.when(has_down)
    def _():
        for copy in to_down:
            copy.start()

    tile = (8, LANES)
    lane = iota(tile, 1)
    sub = iota(tile, 0)
    low = lane < per_row

    zeros4 = jnp.zeros((4, columns), jnp.float32)

    @pl.when(jnp.logical_not(has_up))
    def _():
        for ref in (field, east, north):
            ref[rows : rows + 4, :] = zeros4
        col_up[...] = jnp.zeros(tile, jnp.int32)
        use_up[...] = jnp.zeros(tile, jnp.float32)

    @pl.when(jnp.logical_not(has_down))
    def _():
        for ref in (field, east, north):
            ref[rows + 4 : rows + 8, :] = zeros4
        col_down[...] = jnp.zeros(tile, jnp.int32)
        use_down[...] = jnp.zeros(tile, jnp.float32)

    keep = jnp.where((sub >= 4) | has_up, 1.0, 0.0)
    last_lane = lane == LANES - 1
    first_lane = lane == 0
    last_sub = sub == 7
    first_sub = sub == 0

    def block(j):
        return slice(j * LANES, (j + 1) * LANES)

    def get(ref, t, j):
        return ref[8 * t : 8 * t + 8, block(j % blocks)]

    def west_tile(t):
        turned = [pltpu.roll(get(east, t, j), 1, 1) for j in range(blocks)]
        for j in range(blocks):
            west[8 * t : 8 * t + 8, block(j)] = jnp.where(first_lane, turned[j - 1], turned[j])

    def diffuse(source, tiles, coefs, group, finish):
        size = len(tiles)
        for at in range(0, size, group):
            mine = range(at, at + group)
            near = list(mine) if group == size else [(at - 1) % size, *mine, (at + group) % size]
            ahead = {k: pltpu.roll(get(source, tiles[k], 0), LANES - 1, 1) for k in mine}
            behind = {k: pltpu.roll(get(source, tiles[k], -1), 1, 1) for k in mine}
            for j in range(blocks):
                vs = [get(source, tiles[k], j) for k in near]
                lifted = [pltpu.roll(v, 7, 0) for v in vs]
                rise = []
                for i in range(len(near) if group == size else len(near) - 1):
                    above = jnp.where(last_sub, lifted[(i + 1) % len(near)], lifted[i])
                    rise.append(get(north, coefs[near[i]], j) * (above - vs[i]))
                sunk = [pltpu.roll(f, 1, 0) for f in rise]
                for i, k in enumerate(mine, 0 if group == size else 1):
                    v = vs[i]
                    turned_east = pltpu.roll(get(source, tiles[k], j + 1), LANES - 1, 1)
                    turned_west = pltpu.roll(v, 1, 1)
                    side = get(east, coefs[k], j) * (jnp.where(last_lane, turned_east, ahead[k]) - v)
                    side = side + get(west, coefs[k], j) * (jnp.where(first_lane, behind[k], turned_west) - v)
                    result = v + (side + (rise[i] - jnp.where(first_sub, sunk[i - 1], sunk[i])))
                    finish(k, j, result * keep if coefs[k] == own else result)
                    ahead[k], behind[k] = turned_east, turned_west

    def into(target):
        def finish(k, j, result):
            target[8 * k : 8 * k + 8, block(j)] = result

        return finish

    inner = list(range(own))
    edge = [own - 1, own, 0]
    flat = [0, 1, 2]

    for load in loads[:3]:
        load.wait()
    for t in range(own):
        west_tile(t)
    diffuse(field, inner, inner, half, into(ping))
    diffuse(ping, inner, inner, half, into(pong))
    diffuse(pong, inner, inner, half, into(ping))
    diffuse(ping, inner, inner, half, into(pong))

    def to_tiles(raw):
        rows_of = rows_int if raw.dtype == jnp.int32 else rows_float
        rows_of[pl.ds(0, rows // 2, stride=2), :] = raw
        rows_of[pl.ds(1, rows // 2, stride=2), :] = pltpu.roll(raw, per_row, 1)
        out = []
        for t in range(half):
            first = rows_of[8 * t : 8 * t + 8, :]
            second = rows_of[8 * (own - 1 - t) : 8 * (own - t), :]
            out.append(jnp.where(low, first, pltpu.roll(second, per_row, 1)))
        return out

    for load in loads[3:7]:
        load.wait()
    raw_shape = (rows // 2, LANES)
    row_at = lat * rows + 2 * iota(raw_shape, 0) + iota(raw_shape, 1) // per_row
    col_raw = cell_raw[...] - row_at * columns
    weight = weight_raw[...]
    for t, value in enumerate(to_tiles(col_raw)):
        col_tile[t] = value
    for t, value in enumerate(to_tiles(col_raw * 4 + kind_raw[...])):
        key_tile[t] = value
    for t, value in enumerate(to_tiles(weight)):
        wgt_tile[t] = value
    for t, value in enumerate(to_tiles(weight * value_raw[...])):
        wv_tile[t] = value

    cols_to_up = halo(3, col_tile.at[0], col_down, up)
    cols_to_down = halo(7, col_tile.at[0], col_up, down)

    @pl.when(has_up)
    def _():
        cols_to_up.start()

    @pl.when(has_down)
    def _():
        cols_to_down.start()

    los = [col_tile[t] & (LANES - 1) for t in range(half)]
    his = [lax.shift_right_logical(col_tile[t], 7) for t in range(half)]
    from_edge = jnp.where(low, sub, 7 - sub) < 4

    def pick(t, first, second):
        found = jnp.zeros(tile, jnp.float32)
        for j in range(blocks):
            got = jnp.where(low, lane_gather(first(j), los[t]), lane_gather(second(j), los[t]))
            found = jnp.where(his[t] == j, got, found)
        return found

    def member_rows(t):
        def rows_at(j):
            pair = member[16 * (t // 2) : 16 * (t // 2) + 16, block(j)].astype(jnp.float32)
            return pair[8 * (t % 2) : 8 * (t % 2) + 8]

        return rows_at

    def rows_of_tile(ref, t):
        return lambda j: get(ref, t, j)

    loads[7].wait()
    for t in range(half):
        member_at[t] = pick(t, member_rows(t), member_rows(own - 1 - t))
    picked = [pick(t, rows_of_tile(pong, t), rows_of_tile(pong, own - 1 - t)) for t in range(half)]
    for t in range(1, half):
        part[t] = member_at[t] * picked[t]

    def stage_copy(t, stage, move, slot):
        return pltpu.make_async_remote_copy(
            src_ref=part.at[stage * half + t], dst_ref=inbox.at[slot],
            send_sem=stage_send.at[slot], recv_sem=stage_recv.at[slot],
            device_id=peer(move), device_id_type=MESH,
        )

    copies = []
    slot = 0
    for t in range(half):
        of_tile = []
        for stage in range(2):
            of_stage = []
            for move in moves(ORDERS[t % len(ORDERS)][stage]):
                of_stage.append((stage_copy(t, stage, move, slot), slot))
                slot += 1
            of_tile.append(of_stage)
        copies.append(of_tile)

    def send(t, stage):
        for copy, _ in copies[t][stage]:
            copy.start()

    def collect(t, stage):
        total = part[stage * half + t]
        for copy, at in copies[t][stage]:
            copy.wait_recv()
            total = total + inbox[at]
        return total

    pl.semaphore_wait(relay, len(moves("x")))
    for t in range(1, half):
        send(t, 0)

    @pl.when(has_up)
    def _():
        for copy in to_down:
            copy.wait_recv()

    @pl.when(has_down)
    def _():
        for copy in to_up:
            copy.wait_recv()

    west_tile(own)
    diffuse(field, edge, edge, 1, into(edge_a))
    diffuse(edge_a, flat, edge, 1, into(edge_b))
    diffuse(edge_b, flat, edge, 1, into(edge_a))
    diffuse(edge_a, flat, edge, 1, into(edge_b))
    picked_edge = pick(0, rows_of_tile(edge_b, 2), rows_of_tile(edge_b, 0))
    part[0] = member_at[0] * jnp.where(from_edge, picked_edge, picked[0])
    send(0, 0)

    half_base = lane & per_row
    in_half = lane & (per_row - 1)

    def merge(i, carry):
        carry = list(carry)
        for u in range(3):
            d = 3 * i + 1 + u
            lanes = half_base | ((lane - d) & (per_row - 1))
            later = in_half >= d
            for t in range(half):
                w0, w1, w2, v0, v1, v2, again = carry[t]
                other = lane_gather(key_tile[t], lanes)
                w = lane_gather(wgt_tile[t], lanes)
                v = lane_gather(wv_tile[t], lanes)
                same = lax.shift_right_logical(other, 2) == col_tile[t]
                kind = other & 3
                m0 = same & (kind == 0)
                m1 = same & (kind == 1)
                m2 = same & (kind == 2)
                carry[t] = (
                    w0 + jnp.where(m0, w, 0.0), w1 + jnp.where(m1, w, 0.0), w2 + jnp.where(m2, w, 0.0),
                    v0 + jnp.where(m0, v, 0.0), v1 + jnp.where(m1, v, 0.0), v2 + jnp.where(m2, v, 0.0),
                    jnp.where(same & later, 1, again),
                )
        return tuple(carry)

    start = []
    for t in range(half):
        kind = key_tile[t] & 3
        start.append(
            tuple(jnp.where(kind == k, wgt_tile[t], 0.0) for k in range(3))
            + tuple(jnp.where(kind == k, wv_tile[t], 0.0) for k in range(3))
            + (jnp.zeros(tile, jnp.int32),)
        )
    merged = lax.fori_loop(0, (per_row - 1) // 3, merge, tuple(start))
    for t in range(half):
        for k in range(6):
            sums[6 * t + k] = merged[t][k]
        rep_tile[t] = jnp.where(merged[t][6] == 0, lane + 1, 0)

    loads[8].wait()

    for t in range(half):
        back_at[t] = pick(t, rows_of_tile(back, t), rows_of_tile(back, own - 1 - t))

    for t in range(1, half):
        total = collect(t, 0)
        part[half + t] = total
        send(t, 1)

    @pl.when(has_up)
    def _():
        cols_to_down.wait_recv()

    @pl.when(has_down)
    def _():
        cols_to_up.wait_recv()

    halo_cols = jnp.where(sub < 4, col_up[...], col_down[...])
    col_tile[half] = halo_cols

    def find_repeat(i, again):
        for u in range(9):
            d = 9 * i + 1 + u
            lanes = half_base | ((lane - d) & (per_row - 1))
            again = jnp.where((lane_gather(halo_cols, lanes) == halo_cols) & (in_half >= d), 1, again)
        return again

    again = lax.fori_loop(0, (per_row - 1) // 9, find_repeat, jnp.zeros(tile, jnp.int32))
    rep_tile[half] = jnp.where(again == 0, lane + 1, 0)

    def spot(t, s):
        col = col_tile[t, pl.ds(s, 1), :]
        rep = rep_tile[t, pl.ds(s, 1), :].astype(jnp.float32)
        hi = lax.shift_right_logical(col, 7)
        lo = col & (LANES - 1)
        ones = jnp.where(iota((LANES, LANES), 0) == lo, 1.0, 0.0).astype(jnp.bfloat16)
        at = jnp.where(iota((blocks, LANES), 0) == hi, rep, 0.0)
        right = iota((blocks, LANES), 1) < per_row
        split = jnp.concatenate([jnp.where(right, at, 0.0), jnp.where(right, 0.0, at)], axis=0).astype(jnp.bfloat16)
        return lax.dot_general(split, ones, (((1,), (1,)), ((), ())), preferred_element_type=jnp.float32)

    def all_rows(i, carry):
        for s in (2 * i, 2 * i + 1):
            for t in range(half):
                found = spot(t, s)
                inverse[t, pl.ds(s, blocks, stride=8), :] = found[:blocks]
                inverse[own - 1 - t, pl.ds(s, blocks, stride=8), :] = found[blocks:]
            found = spot(half, s)
            inverse[own, pl.ds(s, blocks, stride=8), :] = jnp.where(s < 4, found[:blocks], found[blocks:])
        return carry

    lax.fori_loop(0, 4, all_rows, 0)

    part[half] = collect(0, 0)
    send(0, 1)

    def use_of(t):
        s = back_at[t] + collect(t, 1)
        w0, w1, w2, v0, v1, v2 = [sums[6 * t + k] for k in range(6)]
        size = jnp.abs(s)
        small = jnp.exp(-2.0 * size)
        soft = jnp.maximum(2.0 * s, 0.0) + jnp.log1p(small)
        slope = jnp.where(s >= 0, 1.0, small) / (1.0 + small)
        misfit = (w0 * s - v0) + (w1 * (0.5 * s * size) - v1) * size + (w2 * (0.5 * soft) - v2) * slope
        return member_at[t] * misfit

    def place_tile(t, values):
        for j in range(blocks):
            found = inverse[t, 8 * j : 8 * j + 8, :].astype(jnp.int32)
            got = lane_gather(values, jnp.maximum(found - 1, 0))
            ping[8 * t : 8 * t + 8, j * LANES : (j + 1) * LANES] = jnp.where(found > 0, got, 0.0)

    for t in range(1, half):
        use = use_of(t)
        place_tile(t, use)
        place_tile(own - 1 - t, use)

    use = use_of(0)
    use_tile[0] = use
    use_to_up = halo(8, use_tile.at[0], use_down, up)
    use_to_down = halo(9, use_tile.at[0], use_up, down)

    @pl.when(has_up)
    def _():
        use_to_up.start()

    @pl.when(has_down)
    def _():
        use_to_down.start()

    place_tile(0, use)
    place_tile(own - 1, use)

    def to_out(k, j, result):
        out_ref[0, 8 * k : 8 * k + 8, block(j)] = result + get(field, k, j)

    def edge_out(k, j, result):
        t = edge[k]
        if t == own:
            return
        rows_at = slice(8 * t, 8 * t + 8)
        mine = sub < 4 if t == 0 else sub >= 4
        out_ref[0, rows_at, block(j)] = jnp.where(mine, result + get(field, t, j), out_ref[0, rows_at, block(j)])

    diffuse(ping, inner, inner, half, into(pong))
    diffuse(pong, inner, inner, half, into(third))
    diffuse(third, inner, inner, half, into(pong))
    diffuse(pong, inner, inner, half, to_out)

    @pl.when(has_up)
    def _():
        use_to_down.wait_recv()

    @pl.when(has_down)
    def _():
        use_to_up.wait_recv()

    place_tile(own, jnp.where(sub < 4, use_up[...], use_down[...]))
    diffuse(ping, edge, edge, 1, into(edge_a))
    diffuse(edge_a, flat, edge, 1, into(edge_b))
    diffuse(edge_b, flat, edge, 1, into(edge_a))
    diffuse(edge_a, flat, edge, 1, edge_out)

    for of_tile in copies:
        for of_stage in of_tile:
            for copy, _ in of_stage:
                copy.wait_send()

    @pl.when(has_up)
    def _():
        for copy in to_up + [cols_to_up, use_to_up]:
            copy.wait_send()

    @pl.when(has_down)
    def _():
        for copy in to_down + [cols_to_down, use_to_down]:
            copy.wait_send()


def make(mesh, axes=AXES):
    def per_device(ensemble, alpha, background, east_coef, north_coef, obs_cell, obs_type, obs_value, obs_weight):
        rows, columns = background.shape
        blocks = columns // LANES
        own = rows // 8
        half = own // 2
        ext = rows + 8
        packed = (rows // 2, LANES)
        tile = (8, LANES)
        count = dict(axes)
        slots = half * (count["x"] * count["y"] + count["z"] - 2)
        f32, i32 = jnp.float32, jnp.int32
        VMEM = pltpu.VMEM
        scratch = [
            VMEM((ext, columns), f32), VMEM((ext, columns), f32), VMEM((ext, columns), f32), VMEM((ext, columns), f32),
            VMEM((ext, columns), f32), VMEM((ext, columns), f32), VMEM((rows, columns), f32),
            VMEM((24, columns), f32), VMEM((24, columns), f32),
            VMEM((rows, columns), jnp.bfloat16), VMEM((rows, columns), f32),
            VMEM(packed, i32), VMEM(packed, i32), VMEM(packed, f32), VMEM(packed, f32),
            VMEM((rows, LANES), i32), VMEM((rows, LANES), f32),
            VMEM((half + 1, *tile), i32), VMEM((half, *tile), i32), VMEM((half, *tile), f32), VMEM((half, *tile), f32),
            VMEM((6 * half, *tile), f32), VMEM((half, *tile), f32), VMEM((half, *tile), f32),
            VMEM((half + 1, *tile), i32), VMEM((own + 1, 8 * blocks, LANES), f32),
            VMEM(tile, i32), VMEM(tile, i32), VMEM((half, *tile), f32), VMEM(tile, f32), VMEM(tile, f32),
            VMEM((2 * half, *tile), f32), VMEM((slots, *tile), f32),
            pltpu.SemaphoreType.DMA((9,)), pltpu.SemaphoreType.DMA((10,)), pltpu.SemaphoreType.DMA((10,)),
            pltpu.SemaphoreType.DMA((slots,)), pltpu.SemaphoreType.DMA((slots,)), pltpu.SemaphoreType.REGULAR,
        ]
        return pl.pallas_call(
            functools.partial(kernel, axes),
            out_shape=jax.ShapeDtypeStruct((1, rows, columns), f32),
            in_specs=[pl.BlockSpec(memory_space=pltpu.HBM)] * 9,
            out_specs=pl.BlockSpec(memory_space=pltpu.VMEM),
            scratch_shapes=scratch,
            compiler_params=pltpu.CompilerParams(collective_id=0, has_side_effects=True, vmem_limit_bytes=LIMIT),
            name="gradient",
        )(*[pltpu.with_memory_space_constraint(a, pltpu.HBM) for a in (
            alpha, ensemble, background, east_coef, north_coef,
            obs_cell.reshape(packed), obs_type.reshape(packed), obs_value.reshape(packed), obs_weight.reshape(packed),
        )])

    return jax.shard_map(
        per_device,
        mesh=mesh,
        in_specs=(
            P("mem", "lat", None), P("mem", "lat", None), P("lat", None), P("lat", None), P("lat", None),
            P("lat"), P("lat"), P("lat"), P("lat"),
        ),
        out_specs=P("mem", "lat", None),
        check_vma=False,
    )


def solution(mesh):
    return make(mesh)
```

```python
import functools
import itertools

import jax
import jax.numpy as jnp
from jax import lax
from jax.experimental import pallas as pl
from jax.experimental.pallas import tpu as pltpu
from jax.sharding import PartitionSpec as P

PASSES = 4
AXES = (("y", 2), ("x", 4), ("z", 8))
ORDERS = (("z", "xy"), ("xy", "z"), ("z", "xy"), ("xy", "z"))
HOPS = {"y": 4, "x": 1, "z": 1}
LANES = 128
LIMIT = 20 * 2**20
MESH = pl.DeviceIdType.MESH


def iota(shape, dim):
    return lax.broadcasted_iota(jnp.int32, shape, dim)


def lane_gather(values, lanes):
    return jnp.take_along_axis(values, lanes, axis=1, mode="promise_in_bounds")


def kernel(
    axes, alpha_hbm, member_hbm, back_hbm, east_hbm, north_hbm, cell_hbm, kind_hbm, value_hbm, weight_hbm,
    out_ref,
    field, east, north, west, ping, pong, third, edge_a, edge_b, member, back,
    cell_raw, kind_raw, value_raw, weight_raw, rows_int, rows_float,
    col_tile, key_tile, wgt_tile, wv_tile, sums, member_at, back_at, rep_tile, inverse,
    col_up, col_down, use_tile, use_up, use_down, part, inbox,
    load_sem, halo_send, halo_recv, stage_send, stage_recv, relay,
):
    rows = alpha_hbm.shape[1]
    columns = alpha_hbm.shape[2]
    blocks = columns // LANES
    own = rows // 8
    half = own // 2
    per_row = LANES // 2
    loads = [
        pltpu.make_async_copy(source, target, load_sem.at[index])
        for index, (source, target) in enumerate((
            (alpha_hbm.at[0], field.at[pl.ds(0, rows)]), (east_hbm, east.at[pl.ds(0, rows)]),
            (north_hbm, north.at[pl.ds(0, rows)]), (cell_hbm, cell_raw), (kind_hbm, kind_raw),
            (value_hbm, value_raw), (weight_hbm, weight_raw), (member_hbm.at[0], member), (back_hbm, back),
        ))
    ]
    for load in loads[3:8] + loads[:3] + loads[8:]:
        load.start()

    lat = lax.axis_index("lat")
    lats = lax.axis_size("lat")
    mem = lax.axis_index("mem")
    has_up = lat < lats - 1
    has_down = lat > 0

    place = {}
    stride = {}
    rest = mem
    step = 1
    for name, size in reversed(axes):
        place[name] = lax.rem(rest, size)
        stride[name] = step
        rest = rest // size
        step = step * size
    sizes = dict(axes)

    def peer(move):
        to = mem
        for name, ahead in move:
            there = lax.rem(place[name] + ahead, sizes[name])
            to = to + (there - place[name]) * stride[name]
        return {"mem": to, "lat": lat}

    def hops(move):
        return sum(HOPS[name] * min(ahead, sizes[name] - ahead) for name, ahead in move)

    def moves(names):
        every = itertools.product(*[[(name, ahead) for ahead in range(sizes[name])] for name in names])
        return sorted((m for m in every if any(ahead for _, ahead in m)), key=hops, reverse=True)

    up = {"mem": mem, "lat": lat + 1}
    down = {"mem": mem, "lat": lat - 1}

    barrier = pltpu.get_barrier_semaphore()
    met = 0
    for name, size in axes:
        for move in moves(name):
            pl.semaphore_signal(barrier, inc=1, device_id=peer(move), device_id_type=MESH)
            met += 1

    @pl.when(has_up)
    def _():
        pl.semaphore_signal(barrier, inc=1, device_id=up, device_id_type=MESH)

    @pl.when(has_down)
    def _():
        pl.semaphore_signal(barrier, inc=1, device_id=down, device_id_type=MESH)

    pl.semaphore_wait(barrier, met + has_up.astype(jnp.int32) + has_down.astype(jnp.int32))

    for move in moves("x"):
        pl.semaphore_signal(relay, inc=1, device_id=peer(move), device_id_type=MESH)

    def halo(index, source, target, device):
        return pltpu.make_async_remote_copy(
            src_ref=source, dst_ref=target, send_sem=halo_send.at[index], recv_sem=halo_recv.at[index],
            device_id=device, device_id_type=MESH,
        )

    sources = (alpha_hbm.at[0], east_hbm, north_hbm)
    targets = (field, east, north)
    to_up = [
        halo(i, s.at[pl.ds(rows - 4, 4)], t.at[pl.ds(rows + 4, 4)], up)
        for i, (s, t) in enumerate(zip(sources, targets))
    ]
    to_down = [
        halo(4 + i, s.at[pl.ds(0, 4)], t.at[pl.ds(rows, 4)], down)
        for i, (s, t) in enumerate(zip(sources, targets))
    ]

    @pl.when(has_up)
    def _():
        for copy in to_up:
            copy.start()

    @pl.when(has_down)
    def _():
        for copy in to_down:
            copy.start()

    tile = (8, LANES)
    lane = iota(tile, 1)
    sub = iota(tile, 0)
    low = lane < per_row

    zeros4 = jnp.zeros((4, columns), jnp.float32)

    @pl.when(jnp.logical_not(has_up))
    def _():
        for ref in (field, east, north):
            ref[rows : rows + 4, :] = zeros4
        col_up[...] = jnp.zeros(tile, jnp.int32)
        use_up[...] = jnp.zeros(tile, jnp.float32)

    @pl.when(jnp.logical_not(has_down))
    def _():
        for ref in (field, east, north):
            ref[rows + 4 : rows + 8, :] = zeros4
        col_down[...] = jnp.zeros(tile, jnp.int32)
        use_down[...] = jnp.zeros(tile, jnp.float32)

    keep = jnp.where((sub >= 4) | has_up, 1.0, 0.0)
    last_lane = lane == LANES - 1
    first_lane = lane == 0
    last_sub = sub == 7
    first_sub = sub == 0

    def block(j):
        return slice(j * LANES, (j + 1) * LANES)

    def get(ref, t, j):
        return ref[8 * t : 8 * t + 8, block(j % blocks)]

    def west_tile(t):
        turned = [pltpu.roll(get(east, t, j), 1, 1) for j in range(blocks)]
        for j in range(blocks):
            west[8 * t : 8 * t + 8, block(j)] = jnp.where(first_lane, turned[j - 1], turned[j])

    def diffuse(source, tiles, coefs, group, finish):
        size = len(tiles)
        for at in range(0, size, group):
            mine = range(at, at + group)
            near = list(mine) if group == size else [(at - 1) % size, *mine, (at + group) % size]
            ahead = {k: pltpu.roll(get(source, tiles[k], 0), LANES - 1, 1) for k in mine}
            behind = {k: pltpu.roll(get(source, tiles[k], -1), 1, 1) for k in mine}
            for j in range(blocks):
                vs = [get(source, tiles[k], j) for k in near]
                lifted = [pltpu.roll(v, 7, 0) for v in vs]
                rise = []
                for i in range(len(near) if group == size else len(near) - 1):
                    above = jnp.where(last_sub, lifted[(i + 1) % len(near)], lifted[i])
                    rise.append(get(north, coefs[near[i]], j) * (above - vs[i]))
                sunk = [pltpu.roll(f, 1, 0) for f in rise]
                for i, k in enumerate(mine, 0 if group == size else 1):
                    v = vs[i]
                    turned_east = pltpu.roll(get(source, tiles[k], j + 1), LANES - 1, 1)
                    turned_west = pltpu.roll(v, 1, 1)
                    side = get(east, coefs[k], j) * (jnp.where(last_lane, turned_east, ahead[k]) - v)
                    side = side + get(west, coefs[k], j) * (jnp.where(first_lane, behind[k], turned_west) - v)
                    result = v + (side + (rise[i] - jnp.where(first_sub, sunk[i - 1], sunk[i])))
                    finish(k, j, result * keep if coefs[k] == own else result)
                    ahead[k], behind[k] = turned_east, turned_west

    def into(target):
        def finish(k, j, result):
            target[8 * k : 8 * k + 8, block(j)] = result

        return finish

    inner = list(range(own))
    edge = [own - 1, own, 0]
    flat = [0, 1, 2]

    def to_tiles(raw):
        rows_of = rows_int if raw.dtype == jnp.int32 else rows_float
        rows_of[pl.ds(0, rows // 2, stride=2), :] = raw
        rows_of[pl.ds(1, rows // 2, stride=2), :] = pltpu.roll(raw, per_row, 1)
        out = []
        for t in range(half):
            first = rows_of[8 * t : 8 * t + 8, :]
            second = rows_of[8 * (own - 1 - t) : 8 * (own - t), :]
            out.append(jnp.where(low, first, pltpu.roll(second, per_row, 1)))
        return out

    for load in loads[3:7]:
        load.wait()
    raw_shape = (rows // 2, LANES)
    row_at = lat * rows + 2 * iota(raw_shape, 0) + iota(raw_shape, 1) // per_row
    col_raw = cell_raw[...] - row_at * columns
    weight = weight_raw[...]
    for t, value in enumerate(to_tiles(col_raw)):
        col_tile[t] = value
    for t, value in enumerate(to_tiles(col_raw * 4 + kind_raw[...])):
        key_tile[t] = value
    for t, value in enumerate(to_tiles(weight)):
        wgt_tile[t] = value
    for t, value in enumerate(to_tiles(weight * value_raw[...])):
        wv_tile[t] = value

    cols_to_up = halo(3, col_tile.at[0], col_down, up)
    cols_to_down = halo(7, col_tile.at[0], col_up, down)

    @pl.when(has_up)
    def _():
        cols_to_up.start()

    @pl.when(has_down)
    def _():
        cols_to_down.start()

    los = [col_tile[t] & (LANES - 1) for t in range(half)]
    his = [lax.shift_right_logical(col_tile[t], 7) for t in range(half)]
    from_edge = jnp.where(low, sub, 7 - sub) < 4

    def pick(t, first, second):
        found = jnp.zeros(tile, jnp.float32)
        for j in range(blocks):
            got = jnp.where(low, lane_gather(first(j), los[t]), lane_gather(second(j), los[t]))
            found = jnp.where(his[t] == j, got, found)
        return found

    def member_rows(t):
        def rows_at(j):
            pair = member[16 * (t // 2) : 16 * (t // 2) + 16, block(j)].astype(jnp.float32)
            return pair[8 * (t % 2) : 8 * (t % 2) + 8]

        return rows_at

    def rows_of_tile(ref, t):
        return lambda j: get(ref, t, j)

    loads[7].wait()
    for t in range(half):
        member_at[t] = pick(t, member_rows(t), member_rows(own - 1 - t))
    for load in loads[:3]:
        load.wait()
    for t in range(own):
        west_tile(t)
    diffuse(field, inner, inner, half, into(ping))
    diffuse(ping, inner, inner, half, into(pong))
    diffuse(pong, inner, inner, half, into(ping))
    diffuse(ping, inner, inner, half, into(pong))

    picked = [pick(t, rows_of_tile(pong, t), rows_of_tile(pong, own - 1 - t)) for t in range(half)]
    for t in range(1, half):
        part[t] = member_at[t] * picked[t]

    def stage_copy(t, stage, move, slot):
        return pltpu.make_async_remote_copy(
            src_ref=part.at[stage * half + t], dst_ref=inbox.at[slot],
            send_sem=stage_send.at[slot], recv_sem=stage_recv.at[slot],
            device_id=peer(move), device_id_type=MESH,
        )

    copies = []
    slot = 0
    for t in range(half):
        of_tile = []
        for stage in range(2):
            of_stage = []
            for move in moves(ORDERS[t % len(ORDERS)][stage]):
                of_stage.append((stage_copy(t, stage, move, slot), slot))
                slot += 1
            of_tile.append(of_stage)
        copies.append(of_tile)

    def send(t, stage):
        for copy, _ in copies[t][stage]:
            copy.start()

    def collect(t, stage):
        total = part[stage * half + t]
        for copy, at in copies[t][stage]:
            copy.wait_recv()
            total = total + inbox[at]
        return total

    pl.semaphore_wait(relay, len(moves("x")))
    for t in range(1, half):
        send(t, 0)

    @pl.when(has_up)
    def _():
        for copy in to_down:
            copy.wait_recv()

    @pl.when(has_down)
    def _():
        for copy in to_up:
            copy.wait_recv()

    west_tile(own)
    diffuse(field, edge, edge, 1, into(edge_a))
    diffuse(edge_a, flat, edge, 1, into(edge_b))
    diffuse(edge_b, flat, edge, 1, into(edge_a))
    last = into(edge_b)
    diffuse(edge_a, flat, edge, 1, lambda k, j, result: None if k == 1 else last(k, j, result))
    picked_edge = pick(0, rows_of_tile(edge_b, 2), rows_of_tile(edge_b, 0))
    part[0] = member_at[0] * jnp.where(from_edge, picked_edge, picked[0])
    send(0, 0)

    half_base = lane & per_row
    in_half = lane & (per_row - 1)

    def merge(i, carry):
        carry = list(carry)
        for u in range(3):
            d = 3 * i + 1 + u
            lanes = half_base | ((lane - d) & (per_row - 1))
            later = in_half >= d
            for t in range(half):
                w0, w1, w2, v0, v1, v2, again = carry[t]
                other = lane_gather(key_tile[t], lanes)
                w = lane_gather(wgt_tile[t], lanes)
                v = lane_gather(wv_tile[t], lanes)
                same = lax.shift_right_logical(other, 2) == col_tile[t]
                kind = other & 3
                m0 = same & (kind == 0)
                m1 = same & (kind == 1)
                m2 = same & (kind == 2)
                carry[t] = (
                    w0 + jnp.where(m0, w, 0.0), w1 + jnp.where(m1, w, 0.0), w2 + jnp.where(m2, w, 0.0),
                    v0 + jnp.where(m0, v, 0.0), v1 + jnp.where(m1, v, 0.0), v2 + jnp.where(m2, v, 0.0),
                    jnp.where(same & later, 1, again),
                )
        return tuple(carry)

    start = []
    for t in range(half):
        kind = key_tile[t] & 3
        start.append(
            tuple(jnp.where(kind == k, wgt_tile[t], 0.0) for k in range(3))
            + tuple(jnp.where(kind == k, wv_tile[t], 0.0) for k in range(3))
            + (jnp.zeros(tile, jnp.int32),)
        )
    merged = lax.fori_loop(0, (per_row - 1) // 3, merge, tuple(start))
    for t in range(half):
        for k in range(6):
            sums[6 * t + k] = merged[t][k]
        rep_tile[t] = jnp.where(merged[t][6] == 0, lane + 1, 0)

    loads[8].wait()

    for t in range(half):
        back_at[t] = pick(t, rows_of_tile(back, t), rows_of_tile(back, own - 1 - t))

    @pl.when(has_up)
    def _():
        cols_to_down.wait_recv()

    @pl.when(has_down)
    def _():
        cols_to_up.wait_recv()

    halo_cols = jnp.where(sub < 4, col_up[...], col_down[...])
    col_tile[half] = halo_cols

    def find_repeat(i, again):
        for u in range(9):
            d = 9 * i + 1 + u
            lanes = half_base | ((lane - d) & (per_row - 1))
            again = jnp.where((lane_gather(halo_cols, lanes) == halo_cols) & (in_half >= d), 1, again)
        return again

    again = lax.fori_loop(0, (per_row - 1) // 9, find_repeat, jnp.zeros(tile, jnp.int32))
    rep_tile[half] = jnp.where(again == 0, lane + 1, 0)

    def forward(t):
        part[half + t] = collect(t, 0)
        send(t, 1)

    for t in (2, 0, 1, 3):
        if t < half:
            forward(t)

    def spot(t, s):
        col = col_tile[t, pl.ds(s, 1), :]
        rep = rep_tile[t, pl.ds(s, 1), :].astype(jnp.float32)
        hi = lax.shift_right_logical(col, 7)
        lo = col & (LANES - 1)
        ones = jnp.where(iota((LANES, LANES), 0) == lo, 1.0, 0.0).astype(jnp.bfloat16)
        at = jnp.where(iota((blocks, LANES), 0) == hi, rep, 0.0)
        right = iota((blocks, LANES), 1) < per_row
        split = jnp.concatenate([jnp.where(right, at, 0.0), jnp.where(right, 0.0, at)], axis=0).astype(jnp.bfloat16)
        return lax.dot_general(split, ones, (((1,), (1,)), ((), ())), preferred_element_type=jnp.float32)

    def all_rows(i, carry):
        for s in (2 * i, 2 * i + 1):
            for t in range(half):
                found = spot(t, s)
                inverse[t, pl.ds(s, blocks, stride=8), :] = found[:blocks]
                inverse[own - 1 - t, pl.ds(s, blocks, stride=8), :] = found[blocks:]
            found = spot(half, s)
            inverse[own, pl.ds(s, blocks, stride=8), :] = jnp.where(s < 4, found[:blocks], found[blocks:])
        return carry

    lax.fori_loop(0, 4, all_rows, 0)

    def use_of(t):
        s = back_at[t] + collect(t, 1)
        w0, w1, w2, v0, v1, v2 = [sums[6 * t + k] for k in range(6)]
        size = jnp.abs(s)
        small = jnp.exp(-2.0 * size)
        soft = jnp.maximum(2.0 * s, 0.0) + jnp.log1p(small)
        slope = jnp.where(s >= 0, 1.0, small) / (1.0 + small)
        misfit = (w0 * s - v0) + (w1 * (0.5 * s * size) - v1) * size + (w2 * (0.5 * soft) - v2) * slope
        return member_at[t] * misfit

    def place_tile(t, values):
        for j in range(blocks):
            found = inverse[t, 8 * j : 8 * j + 8, :].astype(jnp.int32)
            got = lane_gather(values, jnp.maximum(found - 1, 0))
            ping[8 * t : 8 * t + 8, j * LANES : (j + 1) * LANES] = jnp.where(found > 0, got, 0.0)

    for t in range(1, half):
        use = use_of(t)
        place_tile(t, use)
        place_tile(own - 1 - t, use)

    use = use_of(0)
    use_tile[0] = use
    use_to_up = halo(8, use_tile.at[0], use_down, up)
    use_to_down = halo(9, use_tile.at[0], use_up, down)

    @pl.when(has_up)
    def _():
        use_to_up.start()

    @pl.when(has_down)
    def _():
        use_to_down.start()

    place_tile(0, use)
    place_tile(own - 1, use)

    def to_out(k, j, result):
        out_ref[0, 8 * k : 8 * k + 8, block(j)] = result + get(field, k, j)

    def edge_out(k, j, result):
        t = edge[k]
        if t == own:
            return
        rows_at = slice(8 * t, 8 * t + 8)
        mine = sub < 4 if t == 0 else sub >= 4
        out_ref[0, rows_at, block(j)] = jnp.where(mine, result + get(field, t, j), out_ref[0, rows_at, block(j)])

    diffuse(ping, inner, inner, half, into(pong))
    diffuse(pong, inner, inner, half, into(third))
    diffuse(third, inner, inner, half, into(pong))
    diffuse(pong, inner, inner, half, to_out)

    @pl.when(has_up)
    def _():
        use_to_down.wait_recv()

    @pl.when(has_down)
    def _():
        use_to_up.wait_recv()

    place_tile(own, jnp.where(sub < 4, use_up[...], use_down[...]))
    diffuse(ping, edge, edge, 1, into(edge_a))
    diffuse(edge_a, flat, edge, 1, into(edge_b))
    diffuse(edge_b, flat, edge, 1, into(edge_a))
    diffuse(edge_a, flat, edge, 1, edge_out)

    for of_tile in copies:
        for of_stage in of_tile:
            for copy, _ in of_stage:
                copy.wait_send()

    @pl.when(has_up)
    def _():
        for copy in to_up + [cols_to_up, use_to_up]:
            copy.wait_send()

    @pl.when(has_down)
    def _():
        for copy in to_down + [cols_to_down, use_to_down]:
            copy.wait_send()


def make(mesh, axes=AXES):
    def per_device(ensemble, alpha, background, east_coef, north_coef, obs_cell, obs_type, obs_value, obs_weight):
        rows, columns = background.shape
        blocks = columns // LANES
        own = rows // 8
        half = own // 2
        ext = rows + 8
        packed = (rows // 2, LANES)
        tile = (8, LANES)
        count = dict(axes)
        slots = half * (count["x"] * count["y"] + count["z"] - 2)
        f32, i32 = jnp.float32, jnp.int32
        VMEM = pltpu.VMEM
        scratch = [
            VMEM((ext, columns), f32), VMEM((ext, columns), f32), VMEM((ext, columns), f32), VMEM((ext, columns), f32),
            VMEM((ext, columns), f32), VMEM((ext, columns), f32), VMEM((rows, columns), f32),
            VMEM((24, columns), f32), VMEM((24, columns), f32),
            VMEM((rows, columns), jnp.bfloat16), VMEM((rows, columns), f32),
            VMEM(packed, i32), VMEM(packed, i32), VMEM(packed, f32), VMEM(packed, f32),
            VMEM((rows, LANES), i32), VMEM((rows, LANES), f32),
            VMEM((half + 1, *tile), i32), VMEM((half, *tile), i32), VMEM((half, *tile), f32), VMEM((half, *tile), f32),
            VMEM((6 * half, *tile), f32), VMEM((half, *tile), f32), VMEM((half, *tile), f32),
            VMEM((half + 1, *tile), i32), VMEM((own + 1, 8 * blocks, LANES), f32),
            VMEM(tile, i32), VMEM(tile, i32), VMEM((half, *tile), f32), VMEM(tile, f32), VMEM(tile, f32),
            VMEM((2 * half, *tile), f32), VMEM((slots, *tile), f32),
            pltpu.SemaphoreType.DMA((9,)), pltpu.SemaphoreType.DMA((10,)), pltpu.SemaphoreType.DMA((10,)),
            pltpu.SemaphoreType.DMA((slots,)), pltpu.SemaphoreType.DMA((slots,)), pltpu.SemaphoreType.REGULAR,
        ]
        return pl.pallas_call(
            functools.partial(kernel, axes),
            out_shape=jax.ShapeDtypeStruct((1, rows, columns), f32),
            in_specs=[pl.BlockSpec(memory_space=pltpu.HBM)] * 9,
            out_specs=pl.BlockSpec(memory_space=pltpu.VMEM),
            scratch_shapes=scratch,
            compiler_params=pltpu.CompilerParams(collective_id=0, has_side_effects=True, vmem_limit_bytes=LIMIT),
            name="gradient",
        )(*[pltpu.with_memory_space_constraint(a, pltpu.HBM) for a in (
            alpha, ensemble, background, east_coef, north_coef,
            obs_cell.reshape(packed), obs_type.reshape(packed), obs_value.reshape(packed), obs_weight.reshape(packed),
        )])

    return jax.shard_map(
        per_device,
        mesh=mesh,
        in_specs=(
            P("mem", "lat", None), P("mem", "lat", None), P("lat", None), P("lat", None), P("lat", None),
            P("lat"), P("lat"), P("lat"), P("lat"),
        ),
        out_specs=P("mem", "lat", None),
        check_vma=False,
    )


def solution(mesh):
    return make(mesh)
```
